32 devices in a mesh: layer: 8 (over z, x), row: 4 (over y, core).
Axes of the slice: x: 2, y: 2, z: 4, core: 2. Of those that a mesh axis runs over, the one named last changes fastest.
Arguments:
- right_side: float32 [8, 1024, 256], P('layer', 'row'), may hold values from -6 to 6
- reduce_factors: float32 [3, 8, 2, 1024, 1024], P(None, 'layer', None, 'row'), may hold values from -0.1875 to 0.1875
- solve_factors: float32 [8, 3, 1024, 1024], P('layer', None, 'row'), may hold values from -0.1875 to 0.1875
Outputs:
- solution: float32 [8, 1024, 256], P('layer', 'row')
The draws below stay inside these ranges and needn't reach their ends.
All inputs are finite; a program needn't handle non-finite values.
Results may differ from the reference program's by a relative error of at most 0.00016.
Values sent between devices are 32-bit elements; how exact they have to be, the bound alone decides.
No kernel may reach another device: no remote copies, remote signals or barrier semaphores. Data moves between devices by JAX's collectives and lax.ppermute only.
A program may use at most 64 MiB of HBM per device.

```python
import jax
import jax.numpy as jnp
from jax import lax

M = 1024
NV = 256
LEVELS = 3
LAYERS = 8


def levels(rng, extent, shards, least, top_value):
    factor_of, own = 1.0, jax.random.fold_in(rng, 6)
    for position, blocks in shards:
        draws = jnp.exp(jax.random.uniform(jax.random.fold_in(own, position), (blocks,), jnp.float32, least / len(shards), top_value / len(shards)))
        factor_of = factor_of * jnp.repeat(draws, extent[position] // blocks).reshape([-1 if axis == position else 1 for axis in range(len(extent))])
    return factor_of


def normal_values(rng, dims, spread, bound, shards=(), held_as=jnp.bfloat16):
    drawn = jax.random.normal(rng, dims, jnp.float32) * spread
    if len(shards) > 0:
        drawn = levels(rng, dims, shards, -0.22, 0.18) * drawn
    return jnp.clip(drawn, min=-bound, max=bound).astype(held_as)


def setup_inputs(seed: int = 0) -> dict:
    arg_keys = jax.random.split(jax.random.key(seed), 4)
    right_side = normal_values(arg_keys[0], (LAYERS, M, NV), 1.0, 6.0, ((0, 8), (1, 4)), jnp.float32)
    reduce_factors = normal_values(arg_keys[1], (LEVELS, LAYERS, 2, M, M), (0.6 * M ** -0.5), 0.1875, ((1, 8), (3, 4)), jnp.float32)
    solve_factors = normal_values(arg_keys[2], (LAYERS, 3, M, M), (M ** -0.5), 0.1875, ((0, 8), (2, 4)), jnp.float32)
    return {"right_side": right_side, "reduce_factors": reduce_factors, "solve_factors": solve_factors}


def apply_blocks(mats, vecs):
    return jnp.einsum("lij,ljn->lin", mats.astype(jnp.float32), vecs.astype(jnp.float32), precision=lax.Precision.HIGHEST)


def reference(right_side, reduce_factors, solve_factors):
    current = right_side
    saved = right_side
    for level_index in range(LEVELS):
        stride = 2 ** level_index
        odd_rows = current[stride::2 * stride]
        saved = saved.at[stride::2 * stride].set(odd_rows)
        lower = jnp.concatenate([jnp.zeros_like(odd_rows[:1]), odd_rows[:-1]], axis=0)
        upper = odd_rows
        kept = current[0::2 * stride]
        lefts = reduce_factors[level_index, 0::2 * stride, 0]
        rights = reduce_factors[level_index, 0::2 * stride, 1]
        kept = kept - apply_blocks(lefts, lower) - apply_blocks(rights, upper)
        current = current.at[0::2 * stride].set(kept)
    saved = saved.at[0].set(current[0])
    base = apply_blocks(solve_factors[:, 0], saved)
    solution = jnp.zeros_like(base).at[0].set(base[0])
    for level_index in reversed(range(LEVELS)):
        stride = 2 ** level_index
        even_rows = solution[0::2 * stride]
        lower = even_rows
        upper = jnp.concatenate([even_rows[1:], jnp.zeros_like(even_rows[:1])], axis=0)
        west = solve_factors[stride::2 * stride, 1]
        east = solve_factors[stride::2 * stride, 2]
        fresh = base[stride::2 * stride] - apply_blocks(west, lower) - apply_blocks(east, upper)
        solution = solution.at[stride::2 * stride].set(fresh)
    return solution
```

```python
import functools

import jax
import jax.numpy as jnp
from jax import lax
from jax.experimental import pallas as pl
from jax.experimental.pallas import tpu as pltpu
from jax.sharding import PartitionSpec as P

AXES = ("layer", "row")
VMEM = pl.BlockSpec(memory_space=pltpu.VMEM)
SMEM = pl.BlockSpec(memory_space=pltpu.SMEM)


def halves(value):
    high = value.astype(jnp.bfloat16)
    return high, (value - high.astype(jnp.float32)).astype(jnp.bfloat16)


def product(left, right):
    left_high, left_low = halves(left)
    right_high, right_low = halves(right)
    dot = functools.partial(jnp.dot, preferred_element_type=jnp.float32)
    return dot(left_high, right_high) + (dot(left_high, right_low) + dot(left_low, right_high))


def combine_kernel(shape, sign, scalar_ref, start_ref, *refs):
    out_ref = refs[-1]
    count = start_ref.shape[0] // 2
    row = scalar_ref[0]
    sums = [start_ref[:count, :], start_ref[count:, :]]
    at = 0
    for pieces in shape:
        mats = refs[at:at + 2]
        at += 2
        for flip, arrivals in pieces:
            piece = refs[at][...]
            for ref in refs[at + 1:at + arrivals]:
                piece = piece + ref[...]
            at += arrivals
            for part in range(2):
                block = row ^ (2 * flip + part)
                columns = pl.ds(pl.multiple_of(block * count, count), count)
                vector = piece[part * count:(part + 1) * count]
                for own in range(2):
                    term = product(mats[own][:, columns], vector)
                    sums[own] = sums[own] + term if sign > 0 else sums[own] - term
    out_ref[:count, :] = sums[0]
    out_ref[count:, :] = sums[1]


def combine(row, start, terms, sign):
    shape, operands = [], []
    for own, sibling, pieces in terms:
        shape.append([(flip, len(arrivals)) for flip, arrivals in pieces])
        operands += [own, sibling]
        for _, arrivals in pieces:
            operands += arrivals
    macs = sum(2 * t[0].size * start.shape[1] for t in terms)
    return pl.pallas_call(
        functools.partial(combine_kernel, shape, sign),
        out_shape=jax.ShapeDtypeStruct(start.shape, start.dtype),
        in_specs=[SMEM] + [VMEM] * (1 + len(operands)),
        out_specs=VMEM,
        cost_estimate=pl.CostEstimate(flops=6 * macs, bytes_accessed=4 * sum(o.size for o in operands), transcendentals=0),
        compiler_params=pltpu.CompilerParams(vmem_limit_bytes=24 << 20),
    )(row, start, *operands)


def on_device(layers, rows, right_side, reduce_factors, solve_factors):
    levels = reduce_factors.shape[0]
    root = layers // 2
    chips = rows // 2
    count, columns = right_side.shape[1], right_side.shape[2] // 2
    layer, row = lax.axis_index("layer"), lax.axis_index("row")
    scalars = row.astype(jnp.int32).reshape(1)
    core = row % 2

    def move(block, pairs, flip=0, swap=0):
        pairs = [(a, b) for a, b in pairs if 0 <= a < layers and 0 <= b < layers]
        if not pairs:
            return None
        hops = [(a * rows + r, b * rows + (r ^ (2 * flip + swap))) for a, b in pairs for r in range(rows)]
        return lax.ppermute(block, AXES, hops)

    def moved(block, pairs, own=True):
        out = []
        for flip in range(0 if own else 1, chips):
            arrived = move(block, pairs, flip)
            if arrived is not None:
                out.append((flip, [arrived]))
        return out

    def both(first, second):
        if not first or not second:
            return first or second
        return [(flip, a + b) for (flip, a), (_, b) in zip(first, second)]

    every = [(i, i) for i in range(layers)]

    mine = lax.dynamic_slice_in_dim(right_side[0], core * columns, columns, 1)
    other = lax.dynamic_slice_in_dim(right_side[0], (1 - core) * columns, columns, 1)
    current = jnp.concatenate([mine, move(other, every, 0, 1)], axis=0)

    sibling_reduce = [move(reduce_factors[k, 0], every, 0, 1) for k in range(levels - 1)]
    sibling_solve = move(solve_factors[0], every, 0, 1)
    own_reduce = [reduce_factors[k, 0] for k in range(levels - 1)]
    own_solve = solve_factors[0]
    root_fold = move(reduce_factors[levels - 1, 0, 1], [(0, root)])
    root_inverse = move(solve_factors[0, 0], [(0, root)])
    root_fold_sibling = move(root_fold, [(root, root)], 0, 1)
    root_inverse_sibling = move(root_inverse, [(root, root)], 0, 1)

    odd = range(1, layers, 2)
    upper = move(current, [(i, i - 1) for i in odd])
    passed = [(flip, move(current, [(i, i + 2) for i in odd], flip)) for flip in range(1, chips)]
    upper_pieces = [(0, [upper])] + moved(upper, [(i - 1, i - 1) for i in odd], own=False)
    lower_pieces = [(0, [move(upper, [(i - 1, i + 1) for i in odd])])]
    lower_pieces += [(flip, [move(block, [(i, i - 1) for i in odd])]) for flip, block in passed]
    current = combine(scalars, current, [
        (own_reduce[0][0], sibling_reduce[0][0], lower_pieces),
        (own_reduce[0][1], sibling_reduce[0][1], upper_pieces),
    ], -1)

    for k in range(1, levels - 1):
        stride = 1 << k
        senders = range(stride, layers, 2 * stride)
        current = combine(scalars, current, [
            (own_reduce[k][0], sibling_reduce[k][0], moved(current, [(i, i + stride) for i in senders])),
            (own_reduce[k][1], sibling_reduce[k][1], moved(current, [(i, i - stride) for i in senders])),
        ], -1)

    first = move(current, [(0, root)])
    saved = [(0, [current])] + moved(current, every, own=False)
    folded = combine(scalars, first, [(root_fold, root_fold_sibling, saved)], -1)
    zero = jnp.zeros_like(current)
    base = combine(scalars, zero, [(own_solve[0], sibling_solve[0], saved)], 1)
    stay = [(root, root)]
    top = combine(scalars, zero, [
        (root_inverse, root_inverse_sibling, [(0, [folded])] + moved(folded, stay, own=False)),
    ], 1)
    middle = combine(scalars, base, [
        (own_solve[1], sibling_solve[1], [(0, [top])] + moved(top, stay, own=False)),
    ], -1)
    top_home = move(top, [(root, 0)])
    result = jnp.where(layer == root, middle, top_home)
    older = top_home

    for k in reversed(range(levels - 1)):
        stride = 1 << k
        late = range(2 * stride, layers, 4 * stride)
        early = range(0, layers, 4 * stride)
        from_early = both(moved(older, [(i, i + stride) for i in early]), moved(older, [(i, i - stride) for i in early]))
        from_late = both(moved(result, [(i, i + stride) for i in late]), moved(result, [(i, i - stride) for i in late]))
        west_late = layer % (4 * stride) == 3 * stride
        target = layer % (2 * stride) == stride
        pick = lambda a, b: jnp.where(west_late, a, b)
        early_own, early_sibling = pick(own_solve[2], own_solve[1]), pick(sibling_solve[2], sibling_solve[1])
        late_own, late_sibling = pick(own_solve[1], own_solve[2]), pick(sibling_solve[1], sibling_solve[2])
        start = combine(scalars, jnp.where(target, base, result), [(early_own, early_sibling, from_early)], -1)
        older = result
        result = combine(scalars, start, [(late_own, late_sibling, from_late)], -1)

    back = move(result[count:], every, 0, 1)
    kept = result[:count]
    return jnp.where(core == 0, jnp.concatenate([kept, back], 1), jnp.concatenate([back, kept], 1))[None]


def solution(mesh):
    placed = (
        P("layer", "row", None),
        P(None, "layer", None, "row", None),
        P("layer", None, "row", None),
    )
    return jax.shard_map(
        functools.partial(on_device, mesh.shape["layer"], mesh.shape["row"]),
        mesh=mesh, in_specs=placed, out_specs=P("layer", "row", None), check_vma=False,
    )
```

```python
import functools

import jax
import jax.numpy as jnp
from jax import lax
from jax.experimental import pallas as pl
from jax.experimental.pallas import tpu as pltpu
from jax.sharding import PartitionSpec as P

AXES = ("layer", "row")
VMEM = pl.BlockSpec(memory_space=pltpu.VMEM)


def halves(value):
    high = value.astype(jnp.bfloat16)
    return high, (value - high.astype(jnp.float32)).astype(jnp.bfloat16)


def product(left, right):
    left_high, left_low = halves(left)
    right_high, right_low = halves(right)
    dot = functools.partial(jnp.dot, preferred_element_type=jnp.float32)
    return dot(left_high, right_high) + (dot(left_high, right_low) + dot(left_low, right_high))


def combine_kernel(shape, sign, level, *refs):
    out_ref = refs[-1]
    count = out_ref.shape[0]
    row = lax.axis_index("row")
    layer = lax.axis_index("layer")
    starts, terms = shape
    if len(starts) == 2:
        total = jnp.where(layer % (2 << level) == (1 << level), refs[starts[0]][...], refs[starts[1]][...])
    else:
        total = refs[starts[0]][...] if starts else None
    for matrix, flip, vector in terms:
        columns = pl.ds(pl.multiple_of((row ^ flip) * count, count), count)
        term = product(refs[matrix][:, columns], refs[vector][...])
        if total is None:
            total = term if sign > 0 else -term
        else:
            total = total + term if sign > 0 else total - term
    out_ref[...] = total


def combine(starts, terms, sign, level=0):
    operands = []

    def place(array):
        for at, known in enumerate(operands):
            if known is array:
                return at
        operands.append(array)
        return len(operands) - 1

    shape = (
        [place(s) for s in starts],
        [(place(matrix), flip, place(vector)) for matrix, flip, vector in terms],
    )
    out = jax.ShapeDtypeStruct(terms[0][2].shape, terms[0][2].dtype)
    return pl.pallas_call(
        functools.partial(combine_kernel, shape, sign, level),
        out_shape=out,
        in_specs=[VMEM] * len(operands),
        out_specs=VMEM,
        cost_estimate=pl.CostEstimate(flops=6 * len(terms) * out.size * out.shape[0], bytes_accessed=0, transcendentals=0),
        compiler_params=pltpu.CompilerParams(vmem_limit_bytes=6 << 20),
    )(*operands)


def load_kernel(levels, reduce_ref, solve_ref, *refs):
    outs, sems = refs[:-1], refs[-1]
    copies = []
    for at, out in enumerate(outs):
        source = reduce_ref.at[at // 2, at % 2] if at < 2 * levels else solve_ref.at[at - 2 * levels]
        copies.append(pltpu.make_async_copy(source, out, sems.at[at]))
    for copy in copies:
        copy.start()
    for copy in copies:
        copy.wait()


def load(reduce_factors, solve_factors):
    levels, shape = reduce_factors.shape[0], reduce_factors.shape[-2:]
    number = 2 * levels + 3
    out = pl.pallas_call(
        functools.partial(load_kernel, levels),
        out_shape=[jax.ShapeDtypeStruct(shape, reduce_factors.dtype)] * number,
        in_specs=[pl.BlockSpec(memory_space=pl.ANY)] * 2,
        out_specs=[VMEM] * number,
        scratch_shapes=[pltpu.SemaphoreType.DMA((number,))],
        cost_estimate=pl.CostEstimate(flops=0, bytes_accessed=0, transcendentals=0),
        compiler_params=pltpu.CompilerParams(vmem_limit_bytes=2 << 20),
    )(reduce_factors, solve_factors)
    return [out[2 * k:2 * k + 2] for k in range(levels)], out[2 * levels:]


def on_device(layers, rows, right_side, reduce_factors, solve_factors):
    levels = reduce_factors.shape[0]
    def move(block, pairs, flip=0):
        hops = [
            (a * rows + r, b * rows + (r ^ flip))
            for a, b in pairs if 0 <= a < layers and 0 <= b < layers for r in range(rows)
        ]
        return lax.ppermute(block, AXES, hops) if hops else None

    def swapped(shards, among=None):
        out = []
        for flip, shard in shards:
            out += [(flip, shard), (flip ^ 1, move(shard, among or every, 1))]
        return out

    def direct(block, pairs):
        return [(flip, move(block, pairs, flip)) for flip in range(0, rows, 2)]

    def within(block, among=None):
        return [(0, block)] + [(flip, move(block, among or every, flip)) for flip in range(2, rows, 2)]

    def apply(starts, sign, *mats_pieces, level=0):
        early = [(m, f, p) for m, ps in mats_pieces for f, p in ps[:2]]
        late = [(m, f, p) for m, ps in mats_pieces for f, p in ps[2:]]
        start = combine(starts, early, sign, level)
        return combine([start], late, sign, level) if late else start

    every = [(i, i) for i in range(layers)]
    current = right_side[0]

    odd = range(1, layers, 2)
    upper = move(current, [(i, i - 1) for i in odd])
    passed = [(flip, move(current, [(i, i + 2) for i in odd], flip)) for flip in range(2, rows, 2)]
    reduce_mats, solve_mats = load(reduce_factors[:, 0], solve_factors[0])
    upper, reduce_mats, solve_mats = lax.optimization_barrier((upper, reduce_mats, solve_mats))
    upper_shards = [(0, upper)] + [(flip, move(upper, [(i - 1, i - 1) for i in odd], flip)) for flip in range(2, rows, 2)]
    lower_shards = [(0, move(upper, [(i - 1, i + 1) for i in odd]))]
    lower_shards += [(flip, move(block, [(i, i - 1) for i in odd])) for flip, block in passed]
    left, right = reduce_mats[0]
    lower, upper = swapped(lower_shards), swapped(upper_shards)
    current = combine([current], [(right, f, p) for f, p in upper[:2]] + [(left, f, p) for f, p in lower[2:]], -1)
    current = combine([current], [(left, f, p) for f, p in lower[:2]] + [(right, f, p) for f, p in upper[2:]], -1)

    inverse, west, east = solve_mats
    for k in range(1, levels - 1):
        stride = 1 << k
        senders = range(stride, layers, 2 * stride)
        left, right = reduce_mats[k]
        lower = swapped(direct(current, [(i, i + stride) for i in senders]))
        upper = swapped(direct(current, [(i, i - stride) for i in senders]))
        current = combine([current], [(left, f, p) for f, p in lower], -1)
        current = combine([current], [(right, f, p) for f, p in upper], -1)

    upper = swapped(direct(current, [(layers // 2, 0)]))
    current = apply([current], -1, (reduce_mats[levels - 1][1], upper))
    base = apply([], 1, (inverse, swapped(within(current))))

    result = base
    for k in reversed(range(levels)):
        stride = 1 << k
        senders = range(0, layers, 2 * stride)
        lower = swapped(direct(result, [(j, j + stride) for j in senders]))
        if k == levels - 1:
            result = apply([base], -1, (west, lower))
        else:
            upper = swapped(direct(result, [(j, j - stride) for j in senders]))
            result = apply([base, result], -1, (west, lower), (east, upper), level=k)
    return result[None]


def solution(mesh):
    placed = (
        P("layer", "row", None),
        P(None, "layer", None, "row", None),
        P("layer", None, "row", None),
    )
    return jax.shard_map(
        functools.partial(on_device, mesh.shape["layer"], mesh.shape["row"]),
        mesh=mesh, in_specs=placed, out_specs=P("layer", "row", None), check_vma=False,
    )
```

```python
import functools

import jax
import jax.numpy as jnp
from jax import lax
from jax.experimental import pallas as pl
from jax.experimental.pallas import tpu as pltpu
from jax.sharding import PartitionSpec as P

AXES = ("layer", "row")
VMEM = pl.BlockSpec(memory_space=pltpu.VMEM)


def halves(value):
    high = value.astype(jnp.bfloat16)
    return high, (value - high.astype(jnp.float32)).astype(jnp.bfloat16)


def product(left, right):
    left_high, left_low = halves(left)
    right_high, right_low = halves(right)
    dot = functools.partial(jnp.dot, preferred_element_type=jnp.float32)
    return dot(left_high, right_high) + (dot(left_high, right_low) + dot(left_low, right_high))


def combine_kernel(shape, sign, only, *refs):
    out_ref = refs[-1]
    count = out_ref.shape[0]
    row = lax.axis_index("row")
    layer = lax.axis_index("layer")
    starts, terms = shape
    total = refs[starts[0]][...] if starts else None
    for matrix, flip, vector, within in terms:
        columns = pl.ds(pl.multiple_of((row ^ flip) * count, count), count)
        term = product(refs[matrix][:, columns], refs[vector][...])
        if within is not None:
            term = jnp.where((layer >= within[0]) & (layer < within[1]), term, 0.0)
        if total is None:
            total = term if sign > 0 else -term
        else:
            total = total + term if sign > 0 else total - term
    if only is not None:
        total = jnp.where(layer % only[0] == only[1], total, refs[starts[-1]][...])
    out_ref[...] = total


def combine(starts, terms, sign, only=None):
    operands = []

    def place(array):
        for at, known in enumerate(operands):
            if known is array:
                return at
        operands.append(array)
        return len(operands) - 1

    shape = (
        [place(s) for s in starts],
        [(place(t[0]), t[1], place(t[2]), t[3] if len(t) > 3 else None) for t in terms],
    )
    out = jax.ShapeDtypeStruct(terms[0][2].shape, terms[0][2].dtype)
    return pl.pallas_call(
        functools.partial(combine_kernel, shape, sign, only),
        out_shape=out,
        in_specs=[VMEM] * len(operands),
        out_specs=VMEM,
        cost_estimate=pl.CostEstimate(flops=6 * len(terms) * out.size * out.shape[0], bytes_accessed=0, transcendentals=0),
        compiler_params=pltpu.CompilerParams(vmem_limit_bytes=6 << 20),
    )(*operands)


def load_kernel(levels, reduce_ref, solve_ref, *refs):
    outs, sems = refs[:-1], refs[-1]
    copies = []
    for at, out in enumerate(outs):
        source = reduce_ref.at[at // 2, at % 2] if at < 2 * levels else solve_ref.at[at - 2 * levels]
        copies.append(pltpu.make_async_copy(source, out, sems.at[at]))
    for copy in copies:
        copy.start()
    for copy in copies:
        copy.wait()


def load(reduce_factors, solve_factors):
    levels, shape = reduce_factors.shape[0], reduce_factors.shape[-2:]
    number = 2 * levels + 3
    out = pl.pallas_call(
        functools.partial(load_kernel, levels),
        out_shape=[jax.ShapeDtypeStruct(shape, reduce_factors.dtype)] * number,
        in_specs=[pl.BlockSpec(memory_space=pl.ANY)] * 2,
        out_specs=[VMEM] * number,
        scratch_shapes=[pltpu.SemaphoreType.DMA((number,))],
        cost_estimate=pl.CostEstimate(flops=0, bytes_accessed=0, transcendentals=0),
        compiler_params=pltpu.CompilerParams(vmem_limit_bytes=2 << 20),
    )(reduce_factors, solve_factors)
    return [out[2 * k:2 * k + 2] for k in range(levels)], out[2 * levels:]


def on_device(layers, rows, right_side, reduce_factors, solve_factors):
    levels = reduce_factors.shape[0]
    def move(block, pairs, flip=0):
        hops = [
            (a * rows + r, b * rows + (r ^ flip))
            for a, b in pairs if 0 <= a < layers and 0 <= b < layers for r in range(rows)
        ]
        return lax.ppermute(block, AXES, hops) if hops else None

    def swapped(shards, among=None):
        out = []
        for flip, shard in shards:
            out += [(flip, shard), (flip ^ 1, move(shard, among or every, 1))]
        return out

    def direct(block, pairs):
        return [(flip, move(block, pairs, flip)) for flip in range(0, rows, 2)]

    def within(block, among=None):
        return [(0, block)] + [(flip, move(block, among or every, flip)) for flip in range(2, rows, 2)]

    def apply(starts, sign, *mats_pieces, only=None):
        early = [(m, f, p) for m, ps in mats_pieces for f, p in ps[:2]]
        late = [(m, f, p) for m, ps in mats_pieces for f, p in ps[2:]]
        start = combine(starts, early, sign, only)
        return combine([start], late, sign, only) if late else start

    def ring(by):
        return [(i, (i + by) % layers) for i in range(layers)]

    every = [(i, i) for i in range(layers)]
    current = right_side[0]

    def hop(block, by):
        return move(block, [(i, i - by) for i in range(1 if by > 0 else 0, layers, 2)])

    def near_shards(near):
        return within(near)

    def far_shards(near, passed, by):
        return [(0, move(near, ring(2 * by)))] + [(flip, hop(shard, by)) for flip, shard in passed]

    upper = hop(current, 1)
    passed = [(flip, move(current, ring(2), flip)) for flip in range(2, rows, 2)]
    reduce_mats, solve_mats = load(reduce_factors[:, 0], solve_factors[0])
    upper, reduce_mats, solve_mats = lax.optimization_barrier((upper, reduce_mats, solve_mats))
    left, right = reduce_mats[0]
    lower, upper = swapped(far_shards(upper, passed, 1)), swapped(near_shards(upper))
    current = combine(
        [current], [(right, f, p) for f, p in upper] + [(left, f, p, (1, layers)) for f, p in lower], -1, (2, 0)
    )

    inverse, west, east = solve_mats
    for k in range(1, levels - 1):
        stride = 1 << k
        senders = range(stride, layers, 2 * stride)
        left, right = reduce_mats[k]
        lower = swapped(direct(current, [(i, i + stride) for i in senders]))
        upper = swapped(direct(current, [(i, i - stride) for i in senders]))
        current = combine([current], [(left, f, p) for f, p in lower], -1)
        current = combine([current], [(right, f, p) for f, p in upper], -1)

    upper = swapped(direct(current, [(layers // 2, 0)]))
    current = apply([current], -1, (reduce_mats[levels - 1][1], upper))
    base = apply([], 1, (inverse, swapped(within(current))))

    result = base
    for k in reversed(range(levels)):
        stride = 1 << k
        only = (2 * stride, stride)
        senders = range(0, layers, 2 * stride)
        if k == levels - 1:
            result = apply([base, result], -1, (west, swapped(direct(result, [(0, stride)]))), only=only)
        elif k > 0:
            lower = swapped(direct(result, [(j, j + stride) for j in senders]))
            upper = swapped(direct(result, [(j, j - stride) for j in senders]))
            result = apply([base, result], -1, (west, lower), (east, upper), only=only)
        else:
            lower = hop(result, -1)
            passed = [(flip, move(result, ring(-2), flip)) for flip in range(2, rows, 2)]
            upper = swapped(far_shards(lower, passed, -1))
            lower = swapped(near_shards(lower))
            result = combine(
                [base, result],
                [(west, f, p) for f, p in lower] + [(east, f, p, (0, layers - 1)) for f, p in upper], -1, only,
            )
    return result[None]


def solution(mesh):
    placed = (
        P("layer", "row", None),
        P(None, "layer", None, "row", None),
        P("layer", None, "row", None),
    )
    return jax.shard_map(
        functools.partial(on_device, mesh.shape["layer"], mesh.shape["row"]),
        mesh=mesh, in_specs=placed, out_specs=P("layer", "row", None), check_vma=False,
    )
```

```python
import functools

import jax
import jax.numpy as jnp
from jax import lax
from jax.experimental import pallas as pl
from jax.experimental.pallas import tpu as pltpu
from jax.sharding import PartitionSpec as P

AXES = ("layer", "row")
VMEM = pl.BlockSpec(memory_space=pltpu.VMEM)


def halves(value):
    high = value.astype(jnp.bfloat16)
    return high, (value - high.astype(jnp.float32)).astype(jnp.bfloat16)


def product(left, right):
    left_high, left_low = halves(left)
    right_high, right_low = halves(right)
    dot = functools.partial(jnp.dot, preferred_element_type=jnp.float32)
    return dot(left_high, right_high) + (dot(left_high, right_low) + dot(left_low, right_high))


def combine_kernel(shape, sign, only, *refs):
    out_ref = refs[-1]
    count = out_ref.shape[0]
    row = lax.axis_index("row")
    layer = lax.axis_index("layer")
    starts, terms = shape
    total = refs[starts[0]][...] if starts else None
    for matrix, flip, vector, within in terms:
        columns = pl.ds(pl.multiple_of((row ^ flip) * count, count), count)
        term = product(refs[matrix][:, columns], refs[vector][...])
        if within is not None:
            term = jnp.where((layer >= within[0]) & (layer < within[1]), term, 0.0)
        if total is None:
            total = term if sign > 0 else -term
        else:
            total = total + term if sign > 0 else total - term
    if only is not None:
        total = jnp.where(layer % only[0] == only[1], total, refs[starts[-1]][...])
    out_ref[...] = total


def combine(starts, terms, sign, only=None):
    operands = []

    def place(array):
        for at, known in enumerate(operands):
            if known is array:
                return at
        operands.append(array)
        return len(operands) - 1

    shape = (
        [place(s) for s in starts],
        [(place(t[0]), t[1], place(t[2]), t[3] if len(t) > 3 else None) for t in terms],
    )
    out = jax.ShapeDtypeStruct(terms[0][2].shape, terms[0][2].dtype)
    return pl.pallas_call(
        functools.partial(combine_kernel, shape, sign, only),
        out_shape=out,
        in_specs=[VMEM] * len(operands),
        out_specs=VMEM,
        cost_estimate=pl.CostEstimate(flops=6 * len(terms) * out.size * out.shape[0], bytes_accessed=0, transcendentals=0),
        compiler_params=pltpu.CompilerParams(vmem_limit_bytes=6 << 20),
    )(*operands)


def load_kernel(levels, reduce_ref, solve_ref, *refs):
    outs, sems = refs[:-1], refs[-1]
    copies = []
    for at, out in enumerate(outs):
        source = reduce_ref.at[at // 2, at % 2] if at < 2 * levels else solve_ref.at[at - 2 * levels]
        copies.append(pltpu.make_async_copy(source, out, sems.at[at]))
    for copy in copies:
        copy.start()
    for copy in copies:
        copy.wait()


def load(reduce_factors, solve_factors):
    levels, shape = reduce_factors.shape[0], reduce_factors.shape[-2:]
    number = 2 * levels + 3
    out = pl.pallas_call(
        functools.partial(load_kernel, levels),
        out_shape=[jax.ShapeDtypeStruct(shape, reduce_factors.dtype)] * number,
        in_specs=[pl.BlockSpec(memory_space=pl.ANY)] * 2,
        out_specs=[VMEM] * number,
        scratch_shapes=[pltpu.SemaphoreType.DMA((number,))],
        cost_estimate=pl.CostEstimate(flops=0, bytes_accessed=0, transcendentals=0),
        compiler_params=pltpu.CompilerParams(vmem_limit_bytes=2 << 20),
    )(reduce_factors, solve_factors)
    return [out[2 * k:2 * k + 2] for k in range(levels)], out[2 * levels:]


def on_device(layers, rows, right_side, reduce_factors, solve_factors):
    levels = reduce_factors.shape[0]
    def move(block, pairs, flip=0):
        hops = [
            (a * rows + r, b * rows + (r ^ flip))
            for a, b in pairs if 0 <= a < layers and 0 <= b < layers for r in range(rows)
        ]
        return lax.ppermute(block, AXES, hops) if hops else None

    def swapped(shards, among=None):
        out = []
        for flip, shard in shards:
            out += [(flip, shard), (flip ^ 1, move(shard, among or every, 1))]
        return out

    def direct(block, pairs):
        return [(flip, move(block, pairs, flip)) for flip in range(0, rows, 2)]

    def within(block, among=None):
        return [(0, block)] + [(flip, move(block, among or every, flip)) for flip in range(2, rows, 2)]

    def apply(starts, sign, *mats_pieces, only=None, far_first=False):
        early = [(m, f, p) for m, ps in mats_pieces for f, p in ps[:2]]
        late = [(m, f, p) for m, ps in mats_pieces for f, p in ps[2:]]
        if far_first and late:
            early, late = late, early
        start = combine(starts, early, sign, only)
        return combine([start], late, sign, only) if late else start

    def ring(by):
        return [(i, (i + by) % layers) for i in range(layers)]

    every = [(i, i) for i in range(layers)]
    current = right_side[0]

    def hop(block, by):
        return move(block, [(i, i - by) for i in range(1 if by > 0 else 0, layers, 2)])

    def near_shards(near):
        return within(near)

    def far_shards(near, passed, by):
        return [(0, move(near, ring(2 * by)))] + [(flip, hop(shard, by)) for flip, shard in passed]

    upper = hop(current, 1)
    passed = [(flip, move(current, ring(2), flip)) for flip in range(2, rows, 2)]
    reduce_mats, solve_mats = load(reduce_factors[:, 0], solve_factors[0])
    upper, reduce_mats, solve_mats = lax.optimization_barrier((upper, reduce_mats, solve_mats))
    left, right = reduce_mats[0]
    lower, upper = swapped(far_shards(upper, passed, 1)), swapped(near_shards(upper))
    current = combine(
        [current], [(right, f, p) for f, p in upper] + [(left, f, p, (1, layers)) for f, p in lower], -1, (2, 0)
    )

    inverse, west, east = solve_mats
    for k in range(1, levels - 1):
        stride = 1 << k
        senders = range(stride, layers, 2 * stride)
        left, right = reduce_mats[k]
        lower = swapped(direct(current, [(i, i + stride) for i in senders]))
        upper = swapped(direct(current, [(i, i - stride) for i in senders]))
        current = apply([current], -1, (right, upper), (left, lower), far_first=True)

    upper = swapped(direct(current, [(layers // 2, 0)]))
    current = apply([current], -1, (reduce_mats[levels - 1][1], upper), far_first=True)
    base = apply([], 1, (inverse, swapped(within(current))))

    result = base
    for k in reversed(range(levels)):
        stride = 1 << k
        only = (2 * stride, stride)
        senders = range(0, layers, 2 * stride)
        if k == levels - 1:
            result = apply([base, result], -1, (west, swapped(direct(result, [(0, stride)]))), only=only, far_first=True)
        elif k > 0:
            lower = swapped(direct(result, [(j, j + stride) for j in senders]))
            upper = swapped(direct(result, [(j, j - stride) for j in senders]))
            result = apply([base, result], -1, (east, upper), (west, lower), only=only, far_first=True)
        else:
            lower = hop(result, -1)
            passed = [(flip, move(result, ring(-2), flip)) for flip in range(2, rows, 2)]
            upper = swapped(far_shards(lower, passed, -1))
            lower = swapped(near_shards(lower))
            result = combine(
                [base, result],
                [(west, f, p) for f, p in lower] + [(east, f, p, (0, layers - 1)) for f, p in upper], -1, only,
            )
    return result[None]


def solution(mesh):
    placed = (
        P("layer", "row", None),
        P(None, "layer", None, "row", None),
        P("layer", None, "row", None),
    )
    return jax.shard_map(
        functools.partial(on_device, mesh.shape["layer"], mesh.shape["row"]),
        mesh=mesh, in_specs=placed, out_specs=P("layer", "row", None), check_vma=False,
    )
```

```python
import functools

import jax
import jax.numpy as jnp
from jax import lax
from jax.experimental import pallas as pl
from jax.experimental.pallas import tpu as pltpu
from jax.sharding import PartitionSpec as P

AXES = ("layer", "row")
VMEM = pl.BlockSpec(memory_space=pltpu.VMEM)


def halves(value):
    high = value.astype(jnp.bfloat16)
    return high, (value - high.astype(jnp.float32)).astype(jnp.bfloat16)


def product(left, right):
    left_high, left_low = halves(left)
    right_high, right_low = halves(right)
    dot = functools.partial(jnp.dot, preferred_element_type=jnp.float32)
    return dot(left_high, right_high) + (dot(left_high, right_low) + dot(left_low, right_high))


def combine_kernel(shape, sign, only, *refs):
    out_ref = refs[-1]
    count = out_ref.shape[0]
    row = lax.axis_index("row")
    layer = lax.axis_index("layer")
    starts, terms = shape
    total = refs[starts[0]][...] if starts else None
    for matrix, flip, vector, within in terms:
        columns = pl.ds(pl.multiple_of((row ^ flip) * count, count), count)
        term = product(refs[matrix][:, columns], refs[vector][...])
        if within is not None:
            term = jnp.where((layer >= within[0]) & (layer < within[1]), term, 0.0)
        if total is None:
            total = term if sign > 0 else -term
        else:
            total = total + term if sign > 0 else total - term
    if only is not None:
        total = jnp.where(layer % only[0] == only[1], total, refs[starts[-1]][...])
    out_ref[...] = total


def combine(starts, terms, sign, only=None):
    operands = []

    def place(array):
        for at, known in enumerate(operands):
            if known is array:
                return at
        operands.append(array)
        return len(operands) - 1

    shape = (
        [place(s) for s in starts],
        [(place(t[0]), t[1], place(t[2]), t[3] if len(t) > 3 else None) for t in terms],
    )
    out = jax.ShapeDtypeStruct(terms[0][2].shape, terms[0][2].dtype)
    return pl.pallas_call(
        functools.partial(combine_kernel, shape, sign, only),
        out_shape=out,
        in_specs=[VMEM] * len(operands),
        out_specs=VMEM,
        cost_estimate=pl.CostEstimate(flops=6 * len(terms) * out.size * out.shape[0], bytes_accessed=0, transcendentals=0),
        compiler_params=pltpu.CompilerParams(vmem_limit_bytes=6 << 20),
    )(*operands)


def load_kernel(levels, reduce_ref, solve_ref, *refs):
    outs, sems = refs[:-1], refs[-1]
    copies = []
    for at, out in enumerate(outs):
        source = reduce_ref.at[at // 2, at % 2] if at < 2 * levels else solve_ref.at[at - 2 * levels]
        copies.append(pltpu.make_async_copy(source, out, sems.at[at]))
    for copy in copies:
        copy.start()
    for copy in copies:
        copy.wait()


def load(reduce_factors, solve_factors):
    levels, shape = reduce_factors.shape[0], reduce_factors.shape[-2:]
    number = 2 * levels + 3
    out = pl.pallas_call(
        functools.partial(load_kernel, levels),
        out_shape=[jax.ShapeDtypeStruct(shape, reduce_factors.dtype)] * number,
        in_specs=[pl.BlockSpec(memory_space=pl.ANY)] * 2,
        out_specs=[VMEM] * number,
        scratch_shapes=[pltpu.SemaphoreType.DMA((number,))],
        cost_estimate=pl.CostEstimate(flops=0, bytes_accessed=0, transcendentals=0),
        compiler_params=pltpu.CompilerParams(vmem_limit_bytes=2 << 20),
    )(reduce_factors, solve_factors)
    return [out[2 * k:2 * k + 2] for k in range(levels)], out[2 * levels:]


def on_device(layers, rows, right_side, reduce_factors, solve_factors):
    levels = reduce_factors.shape[0]
    def move(block, pairs, flip=0):
        hops = [
            (a * rows + r, b * rows + (r ^ flip))
            for a, b in pairs if 0 <= a < layers and 0 <= b < layers for r in range(rows)
        ]
        return lax.ppermute(block, AXES, hops) if hops else None

    def swapped(shards, among=None):
        out = []
        for flip, shard in shards:
            out += [(flip, shard), (flip ^ 1, move(shard, among or every, 1))]
        return out

    def direct(block, pairs):
        return [(flip, move(block, pairs, flip)) for flip in range(0, rows, 2)]

    def within(block, among=None):
        return [(0, block)] + [(flip, move(block, among or every, flip)) for flip in range(2, rows, 2)]

    def apply(starts, sign, *mats_pieces, only=None, far_first=False):
        early = [(m, f, p) for m, ps in mats_pieces for f, p in ps[:2]]
        late = [(m, f, p) for m, ps in mats_pieces for f, p in ps[2:]]
        if far_first and late:
            early, late = late, early
        start = combine(starts, early, sign, only)
        return combine([start], late, sign, only) if late else start

    def ring(by):
        return [(i, (i + by) % layers) for i in range(layers)]

    every = [(i, i) for i in range(layers)]
    current = right_side[0]

    def hop(block, by):
        return move(block, [(i, i - by) for i in range(1 if by > 0 else 0, layers, 2)])

    def near_shards(near):
        return within(near)

    def far_shards(near, passed, by):
        return [(0, move(near, ring(2 * by)))] + [(flip, hop(shard, by)) for flip, shard in passed]

    upper = hop(current, 1)
    passed = [(flip, move(current, ring(2), flip)) for flip in range(2, rows, 2)]
    reduce_mats, solve_mats = load(reduce_factors[:, 0], solve_factors[0])
    upper, reduce_mats, solve_mats = lax.optimization_barrier((upper, reduce_mats, solve_mats))
    left, right = reduce_mats[0]
    lower, upper = swapped(far_shards(upper, passed, 1)), swapped(near_shards(upper))
    current = combine(
        [current], [(right, f, p) for f, p in upper] + [(left, f, p, (1, layers)) for f, p in lower], -1, (2, 0)
    )

    inverse, west, east = solve_mats
    for k in range(1, levels - 1):
        stride = 1 << k
        senders = range(stride, layers, 2 * stride)
        left, right = reduce_mats[k]
        lower = swapped(direct(current, [(i, i + stride) for i in senders]))
        upper = swapped(direct(current, [(i, i - stride) for i in senders]))
        current = apply([current], -1, (right, upper), (left, lower), far_first=True)

    half = layers // 2
    width = current.shape[1] // 2
    blocks = [current[:, :width], current[:, width:]]
    bases, results = [], []
    for block in blocks:
        upper = swapped(direct(block, [(half, 0)]))
        block = apply([block], -1, (reduce_mats[levels - 1][1], upper), far_first=True)
        base = apply([], 1, (inverse, swapped(within(block))))
        bases.append(base)
        results.append(apply([base, base], -1, (west, swapped(direct(base, [(0, half)]))), only=(2 * half, half), far_first=True))
    base, result = jnp.concatenate(bases, 1), jnp.concatenate(results, 1)

    for k in reversed(range(levels - 1)):
        stride = 1 << k
        only = (2 * stride, stride)
        senders = range(0, layers, 2 * stride)
        if k > 0:
            lower = swapped(direct(result, [(j, j + stride) for j in senders]))
            upper = swapped(direct(result, [(j, j - stride) for j in senders]))
            result = apply([base, result], -1, (east, upper), (west, lower), only=only, far_first=True)
        else:
            lower = hop(result, -1)
            passed = [(flip, move(result, ring(-2), flip)) for flip in range(2, rows, 2)]
            upper = swapped(far_shards(lower, passed, -1))
            lower = swapped(near_shards(lower))
            part = combine(
                [base, result], [(west, f, p) for f, p in lower[:2]] + [(east, f, p, (0, layers - 1)) for f, p in upper[2:]],
                -1, only,
            )
            result = combine(
                [part], [(west, f, p) for f, p in lower[2:]] + [(east, f, p, (0, layers - 1)) for f, p in upper[:2]], -1, only,
            )
    return result[None]


def solution(mesh):
    placed = (
        P("layer", "row", None),
        P(None, "layer", None, "row", None),
        P("layer", None, "row", None),
    )
    return jax.shard_map(
        functools.partial(on_device, mesh.shape["layer"], mesh.shape["row"]),
        mesh=mesh, in_specs=placed, out_specs=P("layer", "row", None), check_vma=False,
    )
```

```python
import functools

import jax
import jax.numpy as jnp
from jax import lax
from jax.experimental import pallas as pl
from jax.experimental.pallas import tpu as pltpu
from jax.sharding import PartitionSpec as P

AXES = ("layer", "row")
VMEM = pl.BlockSpec(memory_space=pltpu.VMEM)


def halves(value):
    high = value.astype(jnp.bfloat16)
    return high, (value - high.astype(jnp.float32)).astype(jnp.bfloat16)


def product(left, right):
    left_high, left_low = halves(left)
    right_high, right_low = halves(right)
    dot = functools.partial(jnp.dot, preferred_element_type=jnp.float32)
    return dot(left_high, right_high) + (dot(left_high, right_low) + dot(left_low, right_high))


def combine_kernel(shape, sign, only, *refs):
    out_ref = refs[-1]
    count = out_ref.shape[0]
    row = lax.axis_index("row")
    layer = lax.axis_index("layer")
    starts, terms = shape
    total = refs[starts[0]][...] if starts else None
    for matrix, flip, vector, within in terms:
        columns = pl.ds(pl.multiple_of((row ^ flip) * count, count), count)
        term = product(refs[matrix][:, columns], refs[vector][...])
        if within is not None:
            term = jnp.where((layer >= within[0]) & (layer < within[1]), term, 0.0)
        if total is None:
            total = term if sign > 0 else -term
        else:
            total = total + term if sign > 0 else total - term
    if only is not None:
        total = jnp.where(layer % only[0] == only[1], total, refs[starts[-1]][...])
    out_ref[...] = total


def combine(starts, terms, sign, only=None):
    operands = []

    def place(array):
        for at, known in enumerate(operands):
            if known is array:
                return at
        operands.append(array)
        return len(operands) - 1

    shape = (
        [place(s) for s in starts],
        [(place(t[0]), t[1], place(t[2]), t[3] if len(t) > 3 else None) for t in terms],
    )
    out = jax.ShapeDtypeStruct(terms[0][2].shape, terms[0][2].dtype)
    return pl.pallas_call(
        functools.partial(combine_kernel, shape, sign, only),
        out_shape=out,
        in_specs=[VMEM] * len(operands),
        out_specs=VMEM,
        cost_estimate=pl.CostEstimate(flops=6 * len(terms) * out.size * out.shape[0], bytes_accessed=0, transcendentals=0),
        compiler_params=pltpu.CompilerParams(vmem_limit_bytes=6 << 20),
    )(*operands)


def load_kernel(levels, reduce_ref, solve_ref, *refs):
    outs, sems = refs[:-1], refs[-1]
    copies = []
    for at, out in enumerate(outs):
        source = reduce_ref.at[at // 2, at % 2] if at < 2 * levels else solve_ref.at[at - 2 * levels]
        copies.append(pltpu.make_async_copy(source, out, sems.at[at]))
    for copy in copies:
        copy.start()
    for copy in copies:
        copy.wait()


def load(reduce_factors, solve_factors):
    levels, shape = reduce_factors.shape[0], reduce_factors.shape[-2:]
    number = 2 * levels + 3
    out = pl.pallas_call(
        functools.partial(load_kernel, levels),
        out_shape=[jax.ShapeDtypeStruct(shape, reduce_factors.dtype)] * number,
        in_specs=[pl.BlockSpec(memory_space=pl.ANY)] * 2,
        out_specs=[VMEM] * number,
        scratch_shapes=[pltpu.SemaphoreType.DMA((number,))],
        cost_estimate=pl.CostEstimate(flops=0, bytes_accessed=0, transcendentals=0),
        compiler_params=pltpu.CompilerParams(vmem_limit_bytes=2 << 20),
    )(reduce_factors, solve_factors)
    return [out[2 * k:2 * k + 2] for k in range(levels)], out[2 * levels:]


def on_device(layers, rows, right_side, reduce_factors, solve_factors):
    levels = reduce_factors.shape[0]
    def move(block, pairs, flip=0):
        hops = [
            (a * rows + r, b * rows + (r ^ flip))
            for a, b in pairs if 0 <= a < layers and 0 <= b < layers for r in range(rows)
        ]
        return lax.ppermute(block, AXES, hops) if hops else None

    def swapped(shards, among=None):
        out = []
        for flip, shard in shards:
            out += [(flip, shard), (flip ^ 1, move(shard, among or every, 1))]
        return out

    def direct(block, pairs):
        return [(flip, move(block, pairs, flip)) for flip in range(0, rows, 2)]

    def traded(block, pairs):
        partner = {a: b for a, b in pairs} | {b: a for a, b in pairs}
        out = []
        for flip in range(0, rows, 2):
            hops = [
                (a * rows + r, partner.get(a, a) * rows + (r ^ (flip if a in partner else 1)))
                for a in range(layers) for r in range(rows)
            ]
            out.append((flip, lax.ppermute(block, AXES, hops)))
        return out

    def within(block, among=None):
        return [(0, block)] + [(flip, move(block, among or every, flip)) for flip in range(2, rows, 2)]

    def apply(starts, sign, *mats_pieces, only=None, far_first=False):
        early = [(m, f, p, *span) for m, ps, *span in mats_pieces for f, p in ps[:2]]
        late = [(m, f, p, *span) for m, ps, *span in mats_pieces for f, p in ps[2:]]
        if far_first and late:
            early, late = late, early
        start = combine(starts, early, sign, only)
        return combine([start], late, sign, only) if late else start

    def ring(by):
        return [(i, (i + by) % layers) for i in range(layers)]

    every = [(i, i) for i in range(layers)]
    current = right_side[0]

    def hop(block, by):
        return move(block, [(i, i - by) for i in range(1 if by > 0 else 0, layers, 2)])

    def near_shards(near):
        return within(near)

    def far_shards(near, passed, by):
        return [(0, move(near, ring(2 * by)))] + [(flip, hop(shard, by)) for flip, shard in passed]

    upper = hop(current, 1)
    passed = [(flip, move(current, ring(2), flip)) for flip in range(2, rows, 2)]
    reduce_mats, solve_mats = load(reduce_factors[:, 0], solve_factors[0])
    upper, reduce_mats, solve_mats = lax.optimization_barrier((upper, reduce_mats, solve_mats))
    left, right = reduce_mats[0]
    lower, upper = swapped(far_shards(upper, passed, 1)), swapped(near_shards(upper))
    current = combine(
        [current], [(right, f, p) for f, p in upper] + [(left, f, p, (1, layers)) for f, p in lower], -1, (2, 0)
    )

    inverse, west, east = solve_mats
    for k in range(1, levels - 1):
        stride = 1 << k
        senders = range(stride, layers, 2 * stride)
        left, right = reduce_mats[k]
        lower = swapped(traded(current, [(i, i + stride) for i in senders if i + stride < layers]))
        upper = swapped(traded(current, [(i, i - stride) for i in senders]))
        current = apply(
            [current], -1, (right, upper), (left, lower, (1, layers)), only=(2 * stride, 0), far_first=True
        )

    half = layers // 2
    width = current.shape[1] // 2
    blocks = [current[:, :width], current[:, width:]]
    bases, results = [], []
    for block in blocks:
        upper = swapped(direct(block, [(half, 0)]))
        block = apply([block], -1, (reduce_mats[levels - 1][1], upper), far_first=True)
        base = apply([], 1, (inverse, swapped(within(block))))
        bases.append(base)
        results.append(apply([base, base], -1, (west, swapped(direct(base, [(0, half)]))), only=(2 * half, half), far_first=True))
    base, result = jnp.concatenate(bases, 1), jnp.concatenate(results, 1)

    for k in reversed(range(levels - 1)):
        stride = 1 << k
        only = (2 * stride, stride)
        senders = range(0, layers, 2 * stride)
        if k > 0:
            lower = swapped(direct(result, [(j, j + stride) for j in senders]))
            upper = swapped(direct(result, [(j, j - stride) for j in senders]))
            result = apply([base, result], -1, (east, upper), (west, lower), only=only, far_first=True)
        else:
            lower = hop(result, -1)
            passed = [(flip, move(result, ring(-2), flip)) for flip in range(2, rows, 2)]
            upper = swapped(far_shards(lower, passed, -1))
            lower = swapped(near_shards(lower))
            part = combine(
                [base, result], [(west, f, p) for f, p in lower[:2]] + [(east, f, p, (0, layers - 1)) for f, p in upper[2:]],
                -1, only,
            )
            result = combine(
                [part], [(west, f, p) for f, p in lower[2:]] + [(east, f, p, (0, layers - 1)) for f, p in upper[:2]], -1, only,
            )
    return result[None]


def solution(mesh):
    placed = (
        P("layer", "row", None),
        P(None, "layer", None, "row", None),
        P("layer", None, "row", None),
    )
    return jax.shard_map(
        functools.partial(on_device, mesh.shape["layer"], mesh.shape["row"]),
        mesh=mesh, in_specs=placed, out_specs=P("layer", "row", None), check_vma=False,
    )
```

```python
import functools

import jax
import jax.numpy as jnp
from jax import lax
from jax.experimental import pallas as pl
from jax.experimental.pallas import tpu as pltpu
from jax.sharding import PartitionSpec as P

AXES = ("layer", "row")
VMEM = pl.BlockSpec(memory_space=pltpu.VMEM)


def halves(value):
    high = value.astype(jnp.bfloat16)
    return high, (value - high.astype(jnp.float32)).astype(jnp.bfloat16)


def product(left, right):
    left_high, left_low = halves(left)
    right_high, right_low = halves(right)
    dot = functools.partial(jnp.dot, preferred_element_type=jnp.float32)
    return dot(left_high, right_high) + (dot(left_high, right_low) + dot(left_low, right_high))


def combine_kernel(shape, sign, only, *refs):
    out_ref = refs[-1]
    count = out_ref.shape[0]
    row = lax.axis_index("row")
    layer = lax.axis_index("layer")
    starts, terms = shape
    total = refs[starts[0]][...] if starts else None
    for matrix, flip, vector, within in terms:
        columns = pl.ds(pl.multiple_of((row ^ flip) * count, count), count)
        term = product(refs[matrix][:, columns], refs[vector][...])
        if within is not None:
            term = jnp.where((layer >= within[0]) & (layer < within[1]), term, 0.0)
        if total is None:
            total = term if sign > 0 else -term
        else:
            total = total + term if sign > 0 else total - term
    if only is not None:
        total = jnp.where(layer % only[0] == only[1], total, refs[starts[-1]][...])
    out_ref[...] = total


def combine(starts, terms, sign, only=None):
    operands = []

    def place(array):
        for at, known in enumerate(operands):
            if known is array:
                return at
        operands.append(array)
        return len(operands) - 1

    shape = (
        [place(s) for s in starts],
        [(place(t[0]), t[1], place(t[2]), t[3] if len(t) > 3 else None) for t in terms],
    )
    out = jax.ShapeDtypeStruct(terms[0][2].shape, terms[0][2].dtype)
    return pl.pallas_call(
        functools.partial(combine_kernel, shape, sign, only),
        out_shape=out,
        in_specs=[VMEM] * len(operands),
        out_specs=VMEM,
        cost_estimate=pl.CostEstimate(flops=6 * len(terms) * out.size * out.shape[0], bytes_accessed=0, transcendentals=0),
        compiler_params=pltpu.CompilerParams(vmem_limit_bytes=6 << 20),
    )(*operands)


def load_kernel(levels, reduce_ref, solve_ref, *refs):
    outs, sems = refs[:-1], refs[-1]
    copies = []
    for at, out in enumerate(outs):
        source = reduce_ref.at[at // 2, at % 2] if at < 2 * levels else solve_ref.at[at - 2 * levels]
        copies.append(pltpu.make_async_copy(source, out, sems.at[at]))
    for copy in copies:
        copy.start()
    for copy in copies:
        copy.wait()


def load(reduce_factors, solve_factors):
    levels, shape = reduce_factors.shape[0], reduce_factors.shape[-2:]
    number = 2 * levels + 3
    out = pl.pallas_call(
        functools.partial(load_kernel, levels),
        out_shape=[jax.ShapeDtypeStruct(shape, reduce_factors.dtype)] * number,
        in_specs=[pl.BlockSpec(memory_space=pl.ANY)] * 2,
        out_specs=[VMEM] * number,
        scratch_shapes=[pltpu.SemaphoreType.DMA((number,))],
        cost_estimate=pl.CostEstimate(flops=0, bytes_accessed=0, transcendentals=0),
        compiler_params=pltpu.CompilerParams(vmem_limit_bytes=2 << 20),
    )(reduce_factors, solve_factors)
    return [out[2 * k:2 * k + 2] for k in range(levels)], out[2 * levels:]


def on_device(layers, rows, right_side, reduce_factors, solve_factors):
    levels = reduce_factors.shape[0]
    def move(block, pairs, flip=0):
        hops = [
            (a * rows + r, b * rows + (r ^ flip))
            for a, b in pairs if 0 <= a < layers and 0 <= b < layers for r in range(rows)
        ]
        return lax.ppermute(block, AXES, hops) if hops else None

    def swapped(shards, among=None):
        out = []
        for flip, shard in shards:
            out += [(flip, shard), (flip ^ 1, move(shard, among or every, 1))]
        return out

    def direct(block, pairs):
        return [(flip, move(block, pairs, flip)) for flip in range(0, rows, 2)]

    def traded(block, pairs):
        partner = {a: b for a, b in pairs} | {b: a for a, b in pairs}
        out = []
        for flip in range(0, rows, 2):
            hops = [
                (a * rows + r, partner.get(a, a) * rows + (r ^ (flip if a in partner else 1)))
                for a in range(layers) for r in range(rows)
            ]
            out.append((flip, lax.ppermute(block, AXES, hops)))
        return out

    def within(block, among=None):
        return [(0, block)] + [(flip, move(block, among or every, flip)) for flip in range(2, rows, 2)]

    def apply(starts, sign, *mats_pieces, only=None, far_first=False):
        early = [(m, f, p, *span) for m, ps, *span in mats_pieces for f, p in ps[:2]]
        late = [(m, f, p, *span) for m, ps, *span in mats_pieces for f, p in ps[2:]]
        if far_first and late:
            early, late = late, early
        start = combine(starts, early, sign, only)
        return combine([start], late, sign, only) if late else start

    def ring(by):
        return [(i, (i + by) % layers) for i in range(layers)]

    every = [(i, i) for i in range(layers)]
    current = right_side[0]

    def hop(block, by):
        return move(block, [(i, i ^ 1) for i in range(layers)])

    def near_shards(near):
        return within(near)

    def far_shards(near, passed, by):
        return [(0, move(near, ring(2 * by)))] + [(flip, hop(shard, by)) for flip, shard in passed]

    upper = hop(current, 1)
    passed = [(flip, move(current, ring(2), flip)) for flip in range(2, rows, 2)]
    reduce_mats, solve_mats = load(reduce_factors[:, 0], solve_factors[0])
    upper, reduce_mats, solve_mats = lax.optimization_barrier((upper, reduce_mats, solve_mats))
    left, right = reduce_mats[0]
    lower, upper = swapped(far_shards(upper, passed, 1)), swapped(near_shards(upper))
    current = combine(
        [current], [(right, f, p) for f, p in upper] + [(left, f, p, (1, layers)) for f, p in lower], -1, (2, 0)
    )

    inverse, west, east = solve_mats
    for k in range(1, levels - 1):
        stride = 1 << k
        senders = range(stride, layers, 2 * stride)
        left, right = reduce_mats[k]
        lower = swapped(traded(current, [(i, i + stride) for i in senders if i + stride < layers]))
        upper = swapped(traded(current, [(i, i - stride) for i in senders]))
        current = apply(
            [current], -1, (right, upper), (left, lower, (1, layers)), only=(2 * stride, 0), far_first=True
        )

    half = layers // 2
    width = current.shape[1] // 2
    blocks = [current[:, :width], current[:, width:]]
    bases, results = [], []
    for block in blocks:
        upper = swapped(direct(block, [(half, 0)]))
        block = apply([block], -1, (reduce_mats[levels - 1][1], upper), far_first=True)
        base = apply([], 1, (inverse, swapped(within(block))))
        bases.append(base)
        results.append(apply([base, base], -1, (west, swapped(direct(base, [(0, half)]))), only=(2 * half, half), far_first=True))
    base, result = jnp.concatenate(bases, 1), jnp.concatenate(results, 1)

    for k in reversed(range(levels - 1)):
        stride = 1 << k
        only = (2 * stride, stride)
        senders = range(0, layers, 2 * stride)
        if k > 0:
            lower = swapped(direct(result, [(j, j + stride) for j in senders]))
            upper = swapped(direct(result, [(j, j - stride) for j in senders]))
            result = apply([base, result], -1, (east, upper), (west, lower), only=only, far_first=True)
        else:
            lower = hop(result, -1)
            passed = [(flip, move(result, ring(-2), flip)) for flip in range(2, rows, 2)]
            upper = swapped(far_shards(lower, passed, -1))
            lower = swapped(near_shards(lower))
            part = combine(
                [base, result], [(west, f, p) for f, p in lower[:2]] + [(east, f, p, (0, layers - 1)) for f, p in upper[2:]],
                -1, only,
            )
            result = combine(
                [part], [(west, f, p) for f, p in lower[2:]] + [(east, f, p, (0, layers - 1)) for f, p in upper[:2]], -1, only,
            )
    return result[None]


def solution(mesh):
    placed = (
        P("layer", "row", None),
        P(None, "layer", None, "row", None),
        P("layer", None, "row", None),
    )
    return jax.shard_map(
        functools.partial(on_device, mesh.shape["layer"], mesh.shape["row"]),
        mesh=mesh, in_specs=placed, out_specs=P("layer", "row", None), check_vma=False,
    )
```

```python
import functools

import jax
import jax.numpy as jnp
from jax import lax
from jax.experimental import pallas as pl
from jax.experimental.pallas import tpu as pltpu
from jax.sharding import PartitionSpec as P

AXES = ("layer", "row")
VMEM = pl.BlockSpec(memory_space=pltpu.VMEM)


def halves(value):
    high = value.astype(jnp.bfloat16)
    return high, (value - high.astype(jnp.float32)).astype(jnp.bfloat16)


def product(left, right):
    left_high, left_low = halves(left)
    right_high, right_low = halves(right)
    dot = functools.partial(jnp.dot, preferred_element_type=jnp.float32)
    return dot(left_high, right_high) + (dot(left_high, right_low) + dot(left_low, right_high))


def combine_kernel(shape, sign, only, *refs):
    out_ref = refs[-1]
    count = out_ref.shape[0]
    row = lax.axis_index("row")
    layer = lax.axis_index("layer")
    starts, terms = shape
    total = refs[starts[0]][...] if starts else None
    for matrix, flip, vector, within in terms:
        columns = pl.ds(pl.multiple_of((row ^ flip) * count, count), count)
        term = product(refs[matrix][:, columns], refs[vector][...])
        if within is not None:
            term = jnp.where((layer >= within[0]) & (layer < within[1]), term, 0.0)
        if total is None:
            total = term if sign > 0 else -term
        else:
            total = total + term if sign > 0 else total - term
    if only is not None:
        total = jnp.where(layer % only[0] == only[1], total, refs[starts[-1]][...])
    out_ref[...] = total


def combine(starts, terms, sign, only=None):
    operands = []

    def place(array):
        for at, known in enumerate(operands):
            if known is array:
                return at
        operands.append(array)
        return len(operands) - 1

    shape = (
        [place(s) for s in starts],
        [(place(t[0]), t[1], place(t[2]), t[3] if len(t) > 3 else None) for t in terms],
    )
    out = jax.ShapeDtypeStruct(terms[0][2].shape, terms[0][2].dtype)
    return pl.pallas_call(
        functools.partial(combine_kernel, shape, sign, only),
        out_shape=out,
        in_specs=[VMEM] * len(operands),
        out_specs=VMEM,
        cost_estimate=pl.CostEstimate(flops=6 * len(terms) * out.size * out.shape[0], bytes_accessed=0, transcendentals=0),
        compiler_params=pltpu.CompilerParams(vmem_limit_bytes=6 << 20),
    )(*operands)


def load_kernel(levels, reduce_ref, solve_ref, *refs):
    outs, sems = refs[:-1], refs[-1]
    copies = []
    for at, out in enumerate(outs):
        source = reduce_ref.at[at // 2, at % 2] if at < 2 * levels else solve_ref.at[at - 2 * levels]
        copies.append(pltpu.make_async_copy(source, out, sems.at[at]))
    for copy in copies:
        copy.start()
    for copy in copies:
        copy.wait()


def load(reduce_factors, solve_factors):
    levels, shape = reduce_factors.shape[0], reduce_factors.shape[-2:]
    number = 2 * levels + 3
    out = pl.pallas_call(
        functools.partial(load_kernel, levels),
        out_shape=[jax.ShapeDtypeStruct(shape, reduce_factors.dtype)] * number,
        in_specs=[pl.BlockSpec(memory_space=pl.ANY)] * 2,
        out_specs=[VMEM] * number,
        scratch_shapes=[pltpu.SemaphoreType.DMA((number,))],
        cost_estimate=pl.CostEstimate(flops=0, bytes_accessed=0, transcendentals=0),
        compiler_params=pltpu.CompilerParams(vmem_limit_bytes=2 << 20),
    )(reduce_factors, solve_factors)
    return [out[2 * k:2 * k + 2] for k in range(levels)], out[2 * levels:]


def on_device(layers, rows, right_side, reduce_factors, solve_factors):
    levels = reduce_factors.shape[0]
    def move(block, pairs, flip=0):
        hops = [
            (a * rows + r, b * rows + (r ^ flip))
            for a, b in pairs if 0 <= a < layers and 0 <= b < layers for r in range(rows)
        ]
        return lax.ppermute(block, AXES, hops) if hops else None

    def swapped(shards, among=None):
        out = []
        for flip, shard in shards:
            out += [(flip, shard), (flip ^ 1, move(shard, among or every, 1))]
        return out

    def direct(block, pairs):
        return [(flip, move(block, pairs, flip)) for flip in range(0, rows, 2)]

    def traded(block, pairs):
        partner = {a: b for a, b in pairs} | {b: a for a, b in pairs}
        out = []
        for flip in range(0, rows, 2):
            hops = [
                (a * rows + r, partner.get(a, a) * rows + (r ^ (flip if a in partner else 1)))
                for a in range(layers) for r in range(rows)
            ]
            out.append((flip, lax.ppermute(block, AXES, hops)))
        return out

    def within(block, among=None):
        return [(0, block)] + [(flip, move(block, among or every, flip)) for flip in range(2, rows, 2)]

    def apply(starts, sign, *mats_pieces, only=None, far_first=False):
        early = [(m, f, p, *span) for m, ps, *span in mats_pieces for f, p in ps[:2]]
        late = [(m, f, p, *span) for m, ps, *span in mats_pieces for f, p in ps[2:]]
        if far_first and late:
            early, late = late, early
        start = combine(starts, early, sign, only)
        return combine([start], late, sign, only) if late else start

    def ring(by):
        return [(i, (i + by) % layers) for i in range(layers)]

    every = [(i, i) for i in range(layers)]
    current = right_side[0]

    def hop(block, by):
        return move(block, [(i, i ^ 1) for i in range(layers)])

    def near_shards(near):
        return within(near)

    def far_shards(near, passed, by):
        return [(0, move(near, ring(2 * by)))] + [(flip, hop(shard, by)) for flip, shard in passed]

    upper = hop(current, 1)
    passed = [(flip, move(current, ring(2), flip)) for flip in range(2, rows, 2)]
    reduce_mats, solve_mats = load(reduce_factors[:, 0], solve_factors[0])
    upper, reduce_mats, solve_mats = lax.optimization_barrier((upper, reduce_mats, solve_mats))
    left, right = reduce_mats[0]
    lower, upper = swapped(far_shards(upper, passed, 1)), swapped(near_shards(upper))
    current = combine(
        [current], [(right, f, p) for f, p in upper] + [(left, f, p, (1, layers)) for f, p in lower], -1, (2, 0)
    )

    inverse, west, east = solve_mats
    for k in range(1, levels - 1):
        stride = 1 << k
        senders = range(stride, layers, 2 * stride)
        left, right = reduce_mats[k]
        lower = swapped(traded(current, [(i, i + stride) for i in senders if i + stride < layers]))
        upper = swapped(traded(current, [(i, i - stride) for i in senders]))
        current = apply(
            [current], -1, (right, upper), (left, lower, (1, layers)), only=(2 * stride, 0), far_first=True
        )

    half = layers // 2
    width = current.shape[1] // 2
    blocks = [current[:, :width], current[:, width:]]
    bases, results = [], []
    for block in blocks:
        upper = swapped(direct(block, [(half, 0)]))
        block = apply([block], -1, (reduce_mats[levels - 1][1], upper), far_first=True)
        base = apply([], 1, (inverse, swapped(within(block))))
        bases.append(base)
        results.append(apply([base, base], -1, (west, swapped(direct(base, [(0, half)]))), only=(2 * half, half), far_first=True))
    base, result = jnp.concatenate(bases, 1), jnp.concatenate(results, 1)

    for k in reversed(range(levels - 1)):
        stride = 1 << k
        only = (2 * stride, stride)
        senders = range(0, layers, 2 * stride)
        if k > 0:
            lower = swapped(traded(result, [(j, j + stride) for j in senders]))
            upper = swapped(direct(result, [(j, j - stride) for j in senders]))
            result = apply([base, result], -1, (east, upper), (west, lower), only=only, far_first=True)
        else:
            lower = hop(result, -1)
            passed = [(flip, move(result, ring(-2), flip)) for flip in range(2, rows, 2)]
            upper = swapped(far_shards(lower, passed, -1))
            lower = swapped(near_shards(lower))
            part = combine(
                [base, result], [(west, f, p) for f, p in lower[:2]] + [(east, f, p, (0, layers - 1)) for f, p in upper[2:]],
                -1, only,
            )
            result = combine(
                [part], [(west, f, p) for f, p in lower[2:]] + [(east, f, p, (0, layers - 1)) for f, p in upper[:2]], -1, only,
            )
    return result[None]


def solution(mesh):
    placed = (
        P("layer", "row", None),
        P(None, "layer", None, "row", None),
        P("layer", None, "row", None),
    )
    return jax.shard_map(
        functools.partial(on_device, mesh.shape["layer"], mesh.shape["row"]),
        mesh=mesh, in_specs=placed, out_specs=P("layer", "row", None), check_vma=False,
    )
```
